256 devices in a mesh: dp: 16 (over z, core), tensor: 16 (over y, x).
Axes of the slice: x: 4, y: 4, z: 8, core: 2. Of those that a mesh axis runs over, the one named last changes fastest.
Arguments:
- hidden: bfloat16 [8192, 28672], P('dp', 'tensor'), parts along dimension 0, may hold values from -6 to 6
- down_weight: bfloat16 [28672, 4096], P('tensor'), may hold values from -0.03125 to 0.03125
Outputs:
- projected: bfloat16 [8192, 4096], P(('dp', 'tensor')), parts along dimension 0
The draws below stay inside these ranges and needn't reach their ends.
There are 16 independent parts, one for each index of `dp`. The reference program is written for one: setup_inputs(seed, part) draws one part's arguments, and reference() takes and returns one part's arrays. A program takes and returns all parts, laid end to end along the dimension named above; an argument that names none is the same for every part. Nothing has to cross between parts.
All inputs are finite; a program needn't handle non-finite values.
Results may differ from the reference program's by a relative error of at most 0.019.
Values may be sent and summed in bfloat16 or wider, within the bound.
A program may use at most 128 MiB of HBM per device.

```python
import math
import jax
import jax.numpy as jnp
from jax import lax

D = 4096
WALSH = 1024
TOK = 512
FF = 28672
N_TENSOR = 16


def shard_levels(key, extent, pieces, low, largest):
    factor_of = 1.0
    for dim, shards_of in pieces:
        heights = jax.random.uniform(jax.random.fold_in(jax.random.fold_in(key, 6), dim), (shards_of,), jnp.float32, low / len(pieces), largest / len(pieces))
        factor_of = factor_of * jnp.repeat(jnp.exp(heights), extent[dim] // shards_of).reshape((-1,) + (1,) * (len(extent) - 1 - dim))
    return factor_of


def centred(stream_key, shape, spread, bound, shards=(), kind=jnp.bfloat16):
    entries = spread * jax.random.normal(stream_key, shape, jnp.float32)
    if shards:
        entries = entries * shard_levels(stream_key, shape, shards, -0.22, 0.18)
    return jnp.clip(entries, -bound, bound).astype(kind)


def setup_inputs(seed: int = 0, part: int = 0) -> dict:
    splits = jax.random.split(jax.random.key(seed), 3)
    own_keys = jax.random.split(jax.random.fold_in(splits[2], part), 3)
    hidden = centred(own_keys[0], (TOK, FF), 1.0, 6.0, ((1, 16),))
    down_weight = centred(splits[1], (FF, D), FF ** -0.5, 0.03125, ((0, 16),))
    return {"hidden": hidden, "down_weight": down_weight}


def paley_table():
    modulus = 13
    residues = set((number * number % modulus for number in range(1, modulus)))
    legendre = [0.0] + [1.0 if number in residues else -1.0 for number in range(1, modulus)]
    order = modulus + 1
    conference = [[0.0] * order for row_at in range(order)]
    for col_at in range(1, order):
        conference[0][col_at] = 1.0
        conference[col_at][0] = 1.0
    for row_at in range(modulus):
        for col_at in range(modulus):
            conference[row_at + 1][col_at + 1] = legendre[(col_at - row_at) % modulus]
    plus_block = [[1.0, 1.0], [1.0, -1.0]]
    minus_block = [[1.0, -1.0], [-1.0, -1.0]]
    table = [[0.0] * (2 * order) for row_at in range(2 * order)]
    for row_at in range(order):
        for col_at in range(order):
            for inner_row in range(2):
                for inner_col in range(2):
                    value = conference[row_at][col_at] * plus_block[inner_row][inner_col]
                    if row_at == col_at:
                        value = value + minus_block[inner_row][inner_col]
                    table[2 * row_at + inner_row][2 * col_at + inner_col] = value
    return table

def walsh_table(length):
    indices = jnp.arange(length, dtype=jnp.int32)
    common = jnp.bitwise_and(indices[:, None], indices[None, :])
    parity = jnp.zeros((length, length), jnp.int32)
    for position in range(length.bit_length() - 1):
        parity = parity + jnp.bitwise_and(jnp.right_shift(common, position), 1)
    return 1.0 - 2.0 * jnp.bitwise_and(parity, 1).astype(jnp.float32)

def reference(hidden, down_weight):
    walsh = walsh_table(WALSH)
    paley = jnp.asarray(paley_table(), jnp.float32)
    blocks = hidden.astype(jnp.float32).reshape(TOK, WALSH, 28)
    mixed = jnp.einsum('tba,bc->tca', blocks, walsh, precision=lax.Precision.HIGHEST)
    mixed = jnp.einsum('tca,ad->tcd', mixed, paley, precision=lax.Precision.HIGHEST)
    rotated = (mixed * (1.0 / math.sqrt(FF))).reshape(TOK, FF).astype(jnp.bfloat16)
    shard_rows = FF // N_TENSOR
    row_blocks = rotated.reshape(TOK, N_TENSOR, shard_rows).transpose(1, 0, 2)
    weight_blocks = down_weight.reshape(N_TENSOR, shard_rows, D)

    def partial_sum(operands):
        return jnp.dot(operands[0], operands[1], preferred_element_type=jnp.float32).astype(jnp.bfloat16)
    partials = lax.map(partial_sum, (row_blocks, weight_blocks))
    return lax.optimization_barrier(jnp.sum(partials.astype(jnp.float32), axis=0)).astype(jnp.bfloat16)
```

```python
import functools
import math

import jax
import jax.numpy as jnp
import ml_dtypes
import numpy as np
from jax import lax
from jax.experimental import pallas as pl
from jax.experimental.pallas import tpu as pltpu
from jax.sharding import PartitionSpec as P

FF = 28672
SCALE = 1.0 / math.sqrt(FF)
MESH = pl.DeviceIdType.MESH
HALF = 896
ROWS = 16
CHUNKS = 2
QUARTER = 1024


def paley_table():
    modulus = 13
    residues = set(number * number % modulus for number in range(1, modulus))
    legendre = [0.0] + [1.0 if number in residues else -1.0 for number in range(1, modulus)]
    order = modulus + 1
    conference = np.zeros((order, order), np.float32)
    conference[0, 1:] = 1.0
    conference[1:, 0] = 1.0
    for row in range(modulus):
        for col in range(modulus):
            conference[row + 1, col + 1] = legendre[(col - row) % modulus]
    plus_block = np.array([[1.0, 1.0], [1.0, -1.0]], np.float32)
    minus_block = np.array([[1.0, -1.0], [-1.0, -1.0]], np.float32)
    return np.kron(conference, plus_block) + np.kron(np.eye(order, dtype=np.float32), minus_block)


def local_rotation():
    walsh = np.ones((1, 1), np.float32)
    for _ in range(5):
        walsh = np.kron(np.array([[1.0, 1.0], [1.0, -1.0]], np.float32), walsh)
    return np.kron(walsh, paley_table()).astype(ml_dtypes.bfloat16)


def walsh_blocks(values):
    values = list(values)
    apart = 1
    while apart < len(values):
        for low in range(len(values)):
            if low & apart == 0:
                a, b = values[low], values[low + apart]
                values[low], values[low + apart] = a + b, a - b
        apart *= 2
    return values


def kernel(
    hidden, weight, rotation, out,
    w_vmem, k_vmem, mid1, gath, turned, mid2, tokens, product, partial, recv1, recv2, recv3, recv4,
    load_sem, a2a_send, a2a_recv, rs_send, rs_recv,
):
    me = lax.axis_index("tensor")
    y, x = me // 4, me % 4

    def at(y_to, x_to):
        return {"tensor": y_to * 4 + x_to}

    def flip(v, by):
        if by == 1:
            return v + 1 - 2 * (v % 2)
        if by == 3:
            return 3 - v
        return (v + 2) % 4

    barrier = pltpu.get_barrier_semaphore()
    for k in (1, 2, 3):
        pl.semaphore_signal(barrier, inc=1, device_id=at(y, (x + k) % 4), device_id_type=MESH)
        pl.semaphore_signal(barrier, inc=1, device_id=at((y + k) % 4, x), device_id_type=MESH)

    load_k = pltpu.make_async_copy(rotation, k_vmem, load_sem.at[0])
    load_w = pltpu.make_async_copy(weight, w_vmem, load_sem.at[1])

    sends = []

    def push(src, dst, send_sem, recv_sem, to):
        copy = pltpu.make_async_remote_copy(
            src_ref=src, dst_ref=dst, send_sem=send_sem, recv_sem=recv_sem,
            device_id=to, device_id_type=MESH,
        )
        copy.start()

    def landed(buf, sem):
        pltpu.make_async_copy(buf, buf, sem).wait()

    def leg1(turn, c, sources, mid):
        for k in (1, 3, 2, 0):
            for half in (0, 1):
                recv = a2a_recv.at[turn, 0, half, c]
                send = a2a_send.at[turn, 0, half, c]
                if half == 0:
                    to = (x + k) % 4
                    src, dst, dev = sources(half, c).at[:, to], mid.at[half, c, x], at(y, to)
                else:
                    to = (y + k) % 4
                    src, dst, dev = sources(half, c).at[to], mid.at[half, c, y], at(to, x)
                if k == 0:
                    pltpu.make_async_copy(src, dst, recv).start()
                else:
                    push(src, dst, send, recv, dev)
        for half in (0, 1):
            sends.append((mid.at[half, c, pl.ds(0, 3)], a2a_send.at[turn, 0, half, c]))

    def leg2(turn, c, mid, end):
        for half in (0, 1):
            landed(mid.at[half, c], a2a_recv.at[turn, 0, half, c])
            for k in (1, 3, 2, 0):
                recv = a2a_recv.at[turn, 1, half, c]
                send = a2a_send.at[turn, 1, half, c]
                if half == 0:
                    to = (y + k) % 4
                    src, dst, dev = mid.at[half, c, :, to], end.at[half, c, y], at(to, x)
                else:
                    to = (x + k) % 4
                    src, dst, dev = mid.at[half, c, :, to], end.at[half, c, :, x], at(y, to)
                if k == 0:
                    pltpu.make_async_copy(src, dst, recv).start()
                else:
                    push(src, dst, send, recv, dev)
            sends.append((mid.at[half, c, pl.ds(0, 3)], a2a_send.at[turn, 1, half, c]))

    def arrive(turn, c, end):
        for half in (0, 1):
            landed(end.at[half, c], a2a_recv.at[turn, 1, half, c])

    def from_hidden(half, c):
        return hidden.at[:, :, pl.ds(ROWS * c, ROWS), pl.ds(HALF * half, HALF)]

    def from_turned(half, c):
        return turned.at[half, c]

    def rotate(c):
        for half in (0, 1):
            block = gath[half, c].reshape(16 * ROWS, HALF)
            product[half] = jnp.dot(block, k_vmem[...], preferred_element_type=jnp.float32)

        def columns(j, carry):
            lanes = pl.ds(pl.multiple_of(j * 128, 128), 128)
            for half in (0, 1):
                values = []
                for s in range(16):
                    a = product[0, pl.ds(s * ROWS, ROWS), lanes]
                    b = product[1, pl.ds(s * ROWS, ROWS), lanes]
                    values.append(a + b if half == 0 else a - b)
                for t, value in enumerate(walsh_blocks(values)):
                    turned[half, c, t // 4, t % 4, :, lanes] = (value * SCALE).astype(jnp.bfloat16)
            return carry

        lax.fori_loop(0, HALF // 128, columns, 0)

    def multiply(c, q):
        def tile(j, carry):
            cols = pl.ds(pl.multiple_of(q * QUARTER + j * 256, 256), 256)
            total = jnp.dot(
                tokens[0, c].reshape(16 * ROWS, HALF), w_vmem[pl.ds(0, HALF), cols],
                preferred_element_type=jnp.float32,
            ) + jnp.dot(
                tokens[1, c].reshape(16 * ROWS, HALF), w_vmem[pl.ds(HALF, HALF), cols],
                preferred_element_type=jnp.float32,
            )
            here = pl.ds(pl.multiple_of(j * 256, 256), 256)
            partial[c, q, :, :, :, here] = total.astype(jnp.bfloat16).reshape(4, 4, ROWS, 256)
            return carry

        lax.fori_loop(0, QUARTER // 256, tile, 0)

    def order(q):
        return (q < 2), ((1, 3) if q % 2 == 0 else (3, 1))

    def peer(along_x, by):
        return at(y, flip(x, by)) if along_x else at(flip(y, by), x)

    def rs1(c, q):
        x_first, (p1, p2) = order(q)
        for slot, by in ((0, p1), (1, 2)):
            src = partial.at[c, q, :, flip(x, by)] if x_first else partial.at[c, q, flip(y, by)]
            push(src, recv1.at[c, q, slot], rs_send.at[c, q, 0], rs_recv.at[c, q, 0], peer(x_first, p1))
        sends.append((recv1.at[c, q], rs_send.at[c, q, 0]))

    def rs2(c, q):
        x_first, (p1, p2) = order(q)
        landed(recv1.at[c, q], rs_recv.at[c, q, 0])
        for slot, by in ((1, p2), (0, 0)):
            pos = flip(x if x_first else y, by) if by else (x if x_first else y)
            ref = partial.at[c, q, :, pos] if x_first else partial.at[c, q, pos]
            ref[...] = (ref[...].astype(jnp.float32) + recv1[c, q, slot].astype(jnp.float32)).astype(jnp.bfloat16)
            if by:
                push(ref, recv2.at[c, q], rs_send.at[c, q, 1], rs_recv.at[c, q, 1], peer(x_first, p2))
                sends.append((recv2.at[c, q], rs_send.at[c, q, 1]))

    def rs3(c, q):
        x_first, (p1, p2) = order(q)
        landed(recv2.at[c, q], rs_recv.at[c, q, 1])
        ref = partial.at[c, q, :, x] if x_first else partial.at[c, q, y]
        ref[...] = (ref[...].astype(jnp.float32) + recv2[c, q].astype(jnp.float32)).astype(jnp.bfloat16)
        for slot, by in ((0, p1), (1, 2)):
            src = partial.at[c, q, flip(y, by), x] if x_first else partial.at[c, q, y, flip(x, by)]
            push(src, recv3.at[c, q, slot], rs_send.at[c, q, 2], rs_recv.at[c, q, 2], peer(not x_first, p1))
        sends.append((recv3.at[c, q], rs_send.at[c, q, 2]))

    def rs4(c, q):
        x_first, (p1, p2) = order(q)
        landed(recv3.at[c, q], rs_recv.at[c, q, 2])
        ref = partial.at[c, q, flip(y, p2), x] if x_first else partial.at[c, q, y, flip(x, p2)]
        ref[...] = (ref[...].astype(jnp.float32) + recv3[c, q, 1].astype(jnp.float32)).astype(jnp.bfloat16)
        push(ref, recv4.at[c, q], rs_send.at[c, q, 3], rs_recv.at[c, q, 3], peer(not x_first, p2))
        sends.append((recv4.at[c, q], rs_send.at[c, q, 3]))

    def finish(c, q):
        landed(recv4.at[c, q], rs_recv.at[c, q, 3])
        total = (
            partial[c, q, y, x].astype(jnp.float32)
            + recv3[c, q, 0].astype(jnp.float32)
            + recv4[c, q].astype(jnp.float32)
        )
        out[pl.ds(ROWS * c, ROWS), pl.ds(QUARTER * q, QUARTER)] = total.astype(jnp.bfloat16)

    pl.semaphore_wait(barrier, 6)
    for c in range(CHUNKS):
        leg1(0, c, from_hidden, mid1)
    load_k.start()
    load_w.start()
    for c in range(CHUNKS):
        leg2(0, c, mid1, gath)
    load_k.wait()
    for c in range(CHUNKS):
        arrive(0, c, gath)
        rotate(c)
        leg1(1, c, from_turned, mid2)
    for c in range(CHUNKS):
        leg2(1, c, mid2, tokens)
    load_w.wait()
    for c in range(CHUNKS):
        arrive(1, c, tokens)
        for q in range(4):
            multiply(c, q)
            rs1(c, q)
    for step in (rs2, rs3, rs4, finish):
        for c in range(CHUNKS):
            for q in range(4):
                step(c, q)
    for ref, sem in sends:
        landed(ref, sem)


def body(hidden, down_weight):
    any_space = pl.BlockSpec(memory_space=pl.ANY)
    legs = (2, CHUNKS, 4, 4, ROWS, HALF)
    bf16 = jnp.bfloat16
    return pl.pallas_call(
        kernel,
        out_shape=jax.ShapeDtypeStruct((32, 4096), bf16),
        in_specs=[any_space] * 3,
        out_specs=pl.BlockSpec(memory_space=pltpu.VMEM),
        scratch_shapes=[
            pltpu.VMEM((2 * HALF, 4096), bf16),
            pltpu.VMEM((HALF, HALF), bf16),
            pltpu.VMEM(legs, bf16),
            pltpu.VMEM(legs, bf16),
            pltpu.VMEM(legs, bf16),
            pltpu.VMEM(legs, bf16),
            pltpu.VMEM(legs, bf16),
            pltpu.VMEM((2, 16 * ROWS, HALF), jnp.float32),
            pltpu.VMEM((CHUNKS, 4, 4, 4, ROWS, QUARTER), bf16),
            pltpu.VMEM((CHUNKS, 4, 2, 4, ROWS, QUARTER), bf16),
            pltpu.VMEM((CHUNKS, 4, 4, ROWS, QUARTER), bf16),
            pltpu.VMEM((CHUNKS, 4, 2, ROWS, QUARTER), bf16),
            pltpu.VMEM((CHUNKS, 4, ROWS, QUARTER), bf16),
            pltpu.SemaphoreType.DMA((2,)),
            pltpu.SemaphoreType.DMA((2, 2, 2, CHUNKS)),
            pltpu.SemaphoreType.DMA((2, 2, 2, CHUNKS)),
            pltpu.SemaphoreType.DMA((CHUNKS, 4, 4)),
            pltpu.SemaphoreType.DMA((CHUNKS, 4, 4)),
        ],
        compiler_params=pltpu.CompilerParams(
            collective_id=0, has_side_effects=True, vmem_limit_bytes=60 << 20
        ),
    )(hidden.reshape(4, 4, 32, 2 * HALF), down_weight, jnp.asarray(local_rotation()))


def solution(mesh):
    placed = (P("dp", "tensor"), P("tensor", None))
    return jax.shard_map(
        body, mesh=mesh, in_specs=placed, out_specs=P(("dp", "tensor"), None), check_vma=False
    )
```

```python
import functools
import math

import jax
import jax.numpy as jnp
import ml_dtypes
import numpy as np
from jax import lax
from jax.experimental import pallas as pl
from jax.experimental.pallas import tpu as pltpu
from jax.sharding import PartitionSpec as P

FF = 28672
SCALE = 1.0 / math.sqrt(FF)
MESH = pl.DeviceIdType.MESH
HALF = 896
ROWS = 16
CHUNKS = 2
PIECES = 8
QUARTER = 4096 // PIECES


def paley_table():
    modulus = 13
    residues = set(number * number % modulus for number in range(1, modulus))
    legendre = [0.0] + [1.0 if number in residues else -1.0 for number in range(1, modulus)]
    order = modulus + 1
    conference = np.zeros((order, order), np.float32)
    conference[0, 1:] = 1.0
    conference[1:, 0] = 1.0
    for row in range(modulus):
        for col in range(modulus):
            conference[row + 1, col + 1] = legendre[(col - row) % modulus]
    plus_block = np.array([[1.0, 1.0], [1.0, -1.0]], np.float32)
    minus_block = np.array([[1.0, -1.0], [-1.0, -1.0]], np.float32)
    return np.kron(conference, plus_block) + np.kron(np.eye(order, dtype=np.float32), minus_block)


def local_rotation():
    walsh = np.ones((1, 1), np.float32)
    for _ in range(5):
        walsh = np.kron(np.array([[1.0, 1.0], [1.0, -1.0]], np.float32), walsh)
    return np.kron(walsh, paley_table()).astype(ml_dtypes.bfloat16)


def walsh_blocks(values):
    values = list(values)
    apart = 1
    while apart < len(values):
        for low in range(len(values)):
            if low & apart == 0:
                a, b = values[low], values[low + apart]
                values[low], values[low + apart] = a + b, a - b
        apart *= 2
    return values


def kernel(
    hidden, weight, rotation, out,
    w_vmem, k_vmem, mid1, gath, turned, mid2, tokens, product, partial, recv1, recv2, recv3, recv4,
    load_sem, a2a_send, a2a_recv, rs_send, rs_recv,
):
    me = lax.axis_index("tensor")
    y, x = me // 4, me % 4

    def at(y_to, x_to):
        return {"tensor": y_to * 4 + x_to}

    def flip(v, by):
        if by == 1:
            return v + 1 - 2 * (v % 2)
        if by == 3:
            return 3 - v
        return (v + 2) % 4

    barrier = pltpu.get_barrier_semaphore()
    for k in (1, 2, 3):
        pl.semaphore_signal(barrier, inc=1, device_id=at(y, (x + k) % 4), device_id_type=MESH)
        pl.semaphore_signal(barrier, inc=1, device_id=at((y + k) % 4, x), device_id_type=MESH)

    load_k = pltpu.make_async_copy(rotation, k_vmem, load_sem.at[0])
    load_w = pltpu.make_async_copy(weight, w_vmem, load_sem.at[1])

    sends = []

    def push(src, dst, send_sem, recv_sem, to):
        copy = pltpu.make_async_remote_copy(
            src_ref=src, dst_ref=dst, send_sem=send_sem, recv_sem=recv_sem,
            device_id=to, device_id_type=MESH,
        )
        copy.start()

    def landed(buf, sem):
        pltpu.make_async_copy(buf, buf, sem).wait()

    def leg1(turn, c, sources, mid):
        for k in (1, 3, 2, 0):
            for half in (0, 1):
                recv = a2a_recv.at[turn, 0, half, c]
                send = a2a_send.at[turn, 0, half, c]
                if half == 0:
                    to = (x + k) % 4
                    src, dst, dev = sources(half, c).at[:, to], mid.at[half, c, x], at(y, to)
                else:
                    to = (y + k) % 4
                    src, dst, dev = sources(half, c).at[to], mid.at[half, c, y], at(to, x)
                if k == 0:
                    pltpu.make_async_copy(src, dst, recv).start()
                else:
                    push(src, dst, send, recv, dev)
        for half in (0, 1):
            sends.append((mid.at[half, c, pl.ds(0, 3)], a2a_send.at[turn, 0, half, c]))

    def leg2(turn, c, mid, end):
        for half in (0, 1):
            landed(mid.at[half, c], a2a_recv.at[turn, 0, half, c])
            for k in (1, 3, 2, 0):
                recv = a2a_recv.at[turn, 1, half, c]
                send = a2a_send.at[turn, 1, half, c]
                if half == 0:
                    to = (y + k) % 4
                    src, dst, dev = mid.at[half, c, :, to], end.at[half, c, y], at(to, x)
                else:
                    to = (x + k) % 4
                    src, dst, dev = mid.at[half, c, :, to], end.at[half, c, :, x], at(y, to)
                if k == 0:
                    pltpu.make_async_copy(src, dst, recv).start()
                else:
                    push(src, dst, send, recv, dev)
            sends.append((mid.at[half, c, pl.ds(0, 3)], a2a_send.at[turn, 1, half, c]))

    def arrive(turn, c, end):
        for half in (0, 1):
            landed(end.at[half, c], a2a_recv.at[turn, 1, half, c])

    def from_hidden(half, c):
        return hidden.at[:, :, pl.ds(ROWS * c, ROWS), pl.ds(HALF * half, HALF)]

    def from_turned(half, c):
        return turned.at[half, c]

    def rotate(c):
        for half in (0, 1):
            block = gath[half, c].reshape(16 * ROWS, HALF)
            product[half] = jnp.dot(block, k_vmem[...], preferred_element_type=jnp.float32)

        def columns(j, carry):
            lanes = pl.ds(pl.multiple_of(j * 128, 128), 128)
            for half in (0, 1):
                values = []
                for s in range(16):
                    a = product[0, pl.ds(s * ROWS, ROWS), lanes]
                    b = product[1, pl.ds(s * ROWS, ROWS), lanes]
                    values.append(a + b if half == 0 else a - b)
                for t, value in enumerate(walsh_blocks(values)):
                    turned[half, c, t // 4, t % 4, :, lanes] = (value * SCALE).astype(jnp.bfloat16)
            return carry

        lax.fori_loop(0, HALF // 128, columns, 0)

    def multiply(c, q):
        def tile(j, carry):
            cols = pl.ds(pl.multiple_of(q * QUARTER + j * 256, 256), 256)
            total = jnp.dot(
                tokens[0, c].reshape(16 * ROWS, HALF), w_vmem[pl.ds(0, HALF), cols],
                preferred_element_type=jnp.float32,
            ) + jnp.dot(
                tokens[1, c].reshape(16 * ROWS, HALF), w_vmem[pl.ds(HALF, HALF), cols],
                preferred_element_type=jnp.float32,
            )
            here = pl.ds(pl.multiple_of(j * 256, 256), 256)
            partial[c, q, :, :, :, here] = total.astype(jnp.bfloat16).reshape(4, 4, ROWS, 256)
            return carry

        lax.fori_loop(0, QUARTER // 256, tile, 0)

    def order(q):
        return (q % 2 == 0), ((1, 3) if q % 4 < 2 else (3, 1))

    def peer(along_x, by):
        return at(y, flip(x, by)) if along_x else at(flip(y, by), x)

    def rs1(c, q):
        x_first, (p1, p2) = order(q)
        for slot, by in ((0, p1), (1, 2)):
            src = partial.at[c, q, :, flip(x, by)] if x_first else partial.at[c, q, flip(y, by)]
            push(src, recv1.at[c, q, slot], rs_send.at[c, q, 0], rs_recv.at[c, q, 0], peer(x_first, p1))
        sends.append((recv1.at[c, q], rs_send.at[c, q, 0]))

    def rs2(c, q):
        x_first, (p1, p2) = order(q)
        landed(recv1.at[c, q], rs_recv.at[c, q, 0])
        for slot, by in ((1, p2), (0, 0)):
            pos = flip(x if x_first else y, by) if by else (x if x_first else y)
            ref = partial.at[c, q, :, pos] if x_first else partial.at[c, q, pos]
            ref[...] = (ref[...].astype(jnp.float32) + recv1[c, q, slot].astype(jnp.float32)).astype(jnp.bfloat16)
            if by:
                push(ref, recv2.at[c, q], rs_send.at[c, q, 1], rs_recv.at[c, q, 1], peer(x_first, p2))
                sends.append((recv2.at[c, q], rs_send.at[c, q, 1]))

    def rs3(c, q):
        x_first, (p1, p2) = order(q)
        landed(recv2.at[c, q], rs_recv.at[c, q, 1])
        ref = partial.at[c, q, :, x] if x_first else partial.at[c, q, y]
        ref[...] = (ref[...].astype(jnp.float32) + recv2[c, q].astype(jnp.float32)).astype(jnp.bfloat16)
        for slot, by in ((0, p1), (1, 2)):
            src = partial.at[c, q, flip(y, by), x] if x_first else partial.at[c, q, y, flip(x, by)]
            push(src, recv3.at[c, q, slot], rs_send.at[c, q, 2], rs_recv.at[c, q, 2], peer(not x_first, p1))
        sends.append((recv3.at[c, q], rs_send.at[c, q, 2]))

    def rs4(c, q):
        x_first, (p1, p2) = order(q)
        landed(recv3.at[c, q], rs_recv.at[c, q, 2])
        ref = partial.at[c, q, flip(y, p2), x] if x_first else partial.at[c, q, y, flip(x, p2)]
        ref[...] = (ref[...].astype(jnp.float32) + recv3[c, q, 1].astype(jnp.float32)).astype(jnp.bfloat16)
        push(ref, recv4.at[c, q], rs_send.at[c, q, 3], rs_recv.at[c, q, 3], peer(not x_first, p2))
        sends.append((recv4.at[c, q], rs_send.at[c, q, 3]))

    def finish(c, q):
        landed(recv4.at[c, q], rs_recv.at[c, q, 3])
        total = (
            partial[c, q, y, x].astype(jnp.float32)
            + recv3[c, q, 0].astype(jnp.float32)
            + recv4[c, q].astype(jnp.float32)
        )
        out[pl.ds(ROWS * c, ROWS), pl.ds(QUARTER * q, QUARTER)] = total.astype(jnp.bfloat16)

    pl.semaphore_wait(barrier, 6)
    for c in range(CHUNKS):
        leg1(0, c, from_hidden, mid1)
    load_k.start()
    load_w.start()
    for c in range(CHUNKS):
        leg2(0, c, mid1, gath)
    load_k.wait()
    for c in range(CHUNKS):
        arrive(0, c, gath)
        rotate(c)
        leg1(1, c, from_turned, mid2)
    for c in range(CHUNKS):
        leg2(1, c, mid2, tokens)
    load_w.wait()
    for c in range(CHUNKS):
        arrive(1, c, tokens)
        for q in range(PIECES):
            multiply(c, q)
            rs1(c, q)
    for step in (rs2, rs3, rs4, finish):
        for c in range(CHUNKS):
            for q in range(PIECES):
                step(c, q)
    for ref, sem in sends:
        landed(ref, sem)


def body(hidden, down_weight):
    any_space = pl.BlockSpec(memory_space=pl.ANY)
    legs = (2, CHUNKS, 4, 4, ROWS, HALF)
    bf16 = jnp.bfloat16
    return pl.pallas_call(
        kernel,
        out_shape=jax.ShapeDtypeStruct((32, 4096), bf16),
        in_specs=[any_space] * 3,
        out_specs=pl.BlockSpec(memory_space=pltpu.VMEM),
        scratch_shapes=[
            pltpu.VMEM((2 * HALF, 4096), bf16),
            pltpu.VMEM((HALF, HALF), bf16),
            pltpu.VMEM(legs, bf16),
            pltpu.VMEM(legs, bf16),
            pltpu.VMEM(legs, bf16),
            pltpu.VMEM(legs, bf16),
            pltpu.VMEM(legs, bf16),
            pltpu.VMEM((2, 16 * ROWS, HALF), jnp.float32),
            pltpu.VMEM((CHUNKS, PIECES, 4, 4, ROWS, QUARTER), bf16),
            pltpu.VMEM((CHUNKS, PIECES, 2, 4, ROWS, QUARTER), bf16),
            pltpu.VMEM((CHUNKS, PIECES, 4, ROWS, QUARTER), bf16),
            pltpu.VMEM((CHUNKS, PIECES, 2, ROWS, QUARTER), bf16),
            pltpu.VMEM((CHUNKS, PIECES, ROWS, QUARTER), bf16),
            pltpu.SemaphoreType.DMA((2,)),
            pltpu.SemaphoreType.DMA((2, 2, 2, CHUNKS)),
            pltpu.SemaphoreType.DMA((2, 2, 2, CHUNKS)),
            pltpu.SemaphoreType.DMA((CHUNKS, PIECES, 4)),
            pltpu.SemaphoreType.DMA((CHUNKS, PIECES, 4)),
        ],
        compiler_params=pltpu.CompilerParams(
            collective_id=0, has_side_effects=True, vmem_limit_bytes=60 << 20
        ),
    )(hidden.reshape(4, 4, 32, 2 * HALF), down_weight, jnp.asarray(local_rotation()))


def solution(mesh):
    placed = (P("dp", "tensor"), P("tensor", None))
    return jax.shard_map(
        body, mesh=mesh, in_specs=placed, out_specs=P(("dp", "tensor"), None), check_vma=False
    )
```

```python
import functools
import math

import jax
import jax.numpy as jnp
import ml_dtypes
import numpy as np
from jax import lax
from jax.experimental import pallas as pl
from jax.experimental.pallas import tpu as pltpu
from jax.sharding import PartitionSpec as P

FF = 28672
SCALE = 1.0 / math.sqrt(FF)
MESH = pl.DeviceIdType.MESH
HALF = 896
ROWS = 16
CHUNKS = 2
PIECES = 8
QUARTER = 4096 // PIECES


def paley_table():
    modulus = 13
    residues = set(number * number % modulus for number in range(1, modulus))
    legendre = [0.0] + [1.0 if number in residues else -1.0 for number in range(1, modulus)]
    order = modulus + 1
    conference = np.zeros((order, order), np.float32)
    conference[0, 1:] = 1.0
    conference[1:, 0] = 1.0
    for row in range(modulus):
        for col in range(modulus):
            conference[row + 1, col + 1] = legendre[(col - row) % modulus]
    plus_block = np.array([[1.0, 1.0], [1.0, -1.0]], np.float32)
    minus_block = np.array([[1.0, -1.0], [-1.0, -1.0]], np.float32)
    return np.kron(conference, plus_block) + np.kron(np.eye(order, dtype=np.float32), minus_block)


def local_rotation():
    walsh = np.ones((1, 1), np.float32)
    for _ in range(5):
        walsh = np.kron(np.array([[1.0, 1.0], [1.0, -1.0]], np.float32), walsh)
    return np.kron(walsh, paley_table()).astype(ml_dtypes.bfloat16)


def walsh_blocks(values):
    values = list(values)
    apart = 1
    while apart < len(values):
        for low in range(len(values)):
            if low & apart == 0:
                a, b = values[low], values[low + apart]
                values[low], values[low + apart] = a + b, a - b
        apart *= 2
    return values


def kernel(
    hidden, weight, rotation, out,
    w_vmem, k_vmem, mid1, gath, turned, mid2, tokens, product, partial, recv1, recv2, recv3, recv4,
    load_sem, a2a_send, a2a_recv, rs_send, rs_recv,
):
    me = lax.axis_index("tensor")
    y, x = me // 4, me % 4

    def at(y_to, x_to):
        return {"tensor": y_to * 4 + x_to}

    def flip(v, by):
        if by == 1:
            return v + 1 - 2 * (v % 2)
        if by == 3:
            return 3 - v
        return (v + 2) % 4

    barrier = pltpu.get_barrier_semaphore()
    for k in (1, 2, 3):
        pl.semaphore_signal(barrier, inc=1, device_id=at(y, (x + k) % 4), device_id_type=MESH)
        pl.semaphore_signal(barrier, inc=1, device_id=at((y + k) % 4, x), device_id_type=MESH)

    load_k = pltpu.make_async_copy(rotation, k_vmem, load_sem.at[0])
    load_w = pltpu.make_async_copy(weight, w_vmem, load_sem.at[1])

    sends = []

    def push(src, dst, send_sem, recv_sem, to):
        copy = pltpu.make_async_remote_copy(
            src_ref=src, dst_ref=dst, send_sem=send_sem, recv_sem=recv_sem,
            device_id=to, device_id_type=MESH,
        )
        copy.start()

    def landed(buf, sem):
        pltpu.make_async_copy(buf, buf, sem).wait()

    def leg1(turn, c, sources, mid):
        for k in (1, 3, 2, 0):
            for half in (0, 1):
                recv = a2a_recv.at[turn, 0, half, c]
                send = a2a_send.at[turn, 0, half, c]
                if half == 0:
                    to = (x + k) % 4
                    src, dst, dev = sources(half, c).at[:, to], mid.at[half, c, x], at(y, to)
                else:
                    to = (y + k) % 4
                    src, dst, dev = sources(half, c).at[to], mid.at[half, c, y], at(to, x)
                if k == 0:
                    pltpu.make_async_copy(src, dst, recv).start()
                else:
                    push(src, dst, send, recv, dev)
        for half in (0, 1):
            sends.append((mid.at[half, c, pl.ds(0, 3)], a2a_send.at[turn, 0, half, c]))

    def leg2(turn, c, mid, end):
        for half in (0, 1):
            landed(mid.at[half, c], a2a_recv.at[turn, 0, half, c])
            for k in (1, 3, 2, 0):
                recv = a2a_recv.at[turn, 1, half, c]
                send = a2a_send.at[turn, 1, half, c]
                if half == 0:
                    to = (y + k) % 4
                    src, dst, dev = mid.at[half, c, :, to], end.at[half, c, y], at(to, x)
                else:
                    to = (x + k) % 4
                    src, dst, dev = mid.at[half, c, :, to], end.at[half, c, :, x], at(y, to)
                if k == 0:
                    pltpu.make_async_copy(src, dst, recv).start()
                else:
                    push(src, dst, send, recv, dev)
            sends.append((mid.at[half, c, pl.ds(0, 3)], a2a_send.at[turn, 1, half, c]))

    def arrive(turn, c, end):
        for half in (0, 1):
            landed(end.at[half, c], a2a_recv.at[turn, 1, half, c])

    def from_hidden(half, c):
        return hidden.at[:, :, pl.ds(ROWS * c, ROWS), pl.ds(HALF * half, HALF)]

    def from_turned(half, c):
        return turned.at[half, c]

    def rotate(c):
        for half in (0, 1):
            block = gath[half, c].reshape(16 * ROWS, HALF)
            product[half] = jnp.dot(block, k_vmem[...], preferred_element_type=jnp.float32)

        def columns(j, carry):
            lanes = pl.ds(pl.multiple_of(j * 128, 128), 128)
            for half in (0, 1):
                values = []
                for s in range(16):
                    a = product[0, pl.ds(s * ROWS, ROWS), lanes]
                    b = product[1, pl.ds(s * ROWS, ROWS), lanes]
                    values.append(a + b if half == 0 else a - b)
                for t, value in enumerate(walsh_blocks(values)):
                    turned[half, c, t // 4, t % 4, :, lanes] = (value * SCALE).astype(jnp.bfloat16)
            return carry

        lax.fori_loop(0, HALF // 128, columns, 0)

    def multiply(c, q):
        def tile(j, carry):
            cols = pl.ds(pl.multiple_of(q * QUARTER + j * 512, 512), 512)
            block = jnp.concatenate([tokens[half, c].reshape(16 * ROWS, HALF) for half in (0, 1)], axis=1)
            total = jnp.dot(block, w_vmem[:, cols], preferred_element_type=jnp.float32)
            here = pl.ds(pl.multiple_of(j * 512, 512), 512)
            partial[c, q, :, :, :, here] = total.astype(jnp.bfloat16).reshape(4, 4, ROWS, 512)
            return carry

        lax.fori_loop(0, QUARTER // 512, tile, 0)

    def order(q):
        return (q % 2 == 0), ((1, 3) if q % 4 < 2 else (3, 1))

    def peer(along_x, by):
        return at(y, flip(x, by)) if along_x else at(flip(y, by), x)

    def rs1(c, q):
        x_first, (p1, p2) = order(q)
        for slot, by in ((0, p1), (1, 2)):
            src = partial.at[c, q, :, flip(x, by)] if x_first else partial.at[c, q, flip(y, by)]
            push(src, recv1.at[c, q, slot], rs_send.at[c, q, 0], rs_recv.at[c, q, 0], peer(x_first, p1))
        sends.append((recv1.at[c, q], rs_send.at[c, q, 0]))

    def rs2(c, q):
        x_first, (p1, p2) = order(q)
        landed(recv1.at[c, q], rs_recv.at[c, q, 0])
        for slot, by in ((1, p2), (0, 0)):
            pos = flip(x if x_first else y, by) if by else (x if x_first else y)
            ref = partial.at[c, q, :, pos] if x_first else partial.at[c, q, pos]
            ref[...] = (ref[...].astype(jnp.float32) + recv1[c, q, slot].astype(jnp.float32)).astype(jnp.bfloat16)
            if by:
                push(ref, recv2.at[c, q], rs_send.at[c, q, 1], rs_recv.at[c, q, 1], peer(x_first, p2))
                sends.append((recv2.at[c, q], rs_send.at[c, q, 1]))

    def rs3(c, q):
        x_first, (p1, p2) = order(q)
        landed(recv2.at[c, q], rs_recv.at[c, q, 1])
        ref = partial.at[c, q, :, x] if x_first else partial.at[c, q, y]
        ref[...] = (ref[...].astype(jnp.float32) + recv2[c, q].astype(jnp.float32)).astype(jnp.bfloat16)
        for slot, by in ((0, p1), (1, 2)):
            src = partial.at[c, q, flip(y, by), x] if x_first else partial.at[c, q, y, flip(x, by)]
            push(src, recv3.at[c, q, slot], rs_send.at[c, q, 2], rs_recv.at[c, q, 2], peer(not x_first, p1))
        sends.append((recv3.at[c, q], rs_send.at[c, q, 2]))

    def rs4(c, q):
        x_first, (p1, p2) = order(q)
        landed(recv3.at[c, q], rs_recv.at[c, q, 2])
        ref = partial.at[c, q, flip(y, p2), x] if x_first else partial.at[c, q, y, flip(x, p2)]
        ref[...] = (ref[...].astype(jnp.float32) + recv3[c, q, 1].astype(jnp.float32)).astype(jnp.bfloat16)
        push(ref, recv4.at[c, q], rs_send.at[c, q, 3], rs_recv.at[c, q, 3], peer(not x_first, p2))
        sends.append((recv4.at[c, q], rs_send.at[c, q, 3]))

    def finish(c, q):
        landed(recv4.at[c, q], rs_recv.at[c, q, 3])
        total = (
            partial[c, q, y, x].astype(jnp.float32)
            + recv3[c, q, 0].astype(jnp.float32)
            + recv4[c, q].astype(jnp.float32)
        )
        out[pl.ds(ROWS * c, ROWS), pl.ds(QUARTER * q, QUARTER)] = total.astype(jnp.bfloat16)

    pl.semaphore_wait(barrier, 6)
    for c in range(CHUNKS):
        leg1(0, c, from_hidden, mid1)
    load_k.start()
    load_w.start()
    for c in range(CHUNKS):
        leg2(0, c, mid1, gath)
    load_k.wait()
    for c in range(CHUNKS):
        arrive(0, c, gath)
        rotate(c)
        leg1(1, c, from_turned, mid2)
    for c in range(CHUNKS):
        leg2(1, c, mid2, tokens)
    load_w.wait()
    for c in range(CHUNKS):
        arrive(1, c, tokens)
        for q in range(PIECES):
            multiply(c, q)
            rs1(c, q)
    for step in (rs2, rs3, rs4, finish):
        for c in range(CHUNKS):
            for q in range(PIECES):
                step(c, q)
    for ref, sem in sends:
        landed(ref, sem)


def body(hidden, down_weight):
    any_space = pl.BlockSpec(memory_space=pl.ANY)
    legs = (2, CHUNKS, 4, 4, ROWS, HALF)
    bf16 = jnp.bfloat16
    return pl.pallas_call(
        kernel,
        out_shape=jax.ShapeDtypeStruct((32, 4096), bf16),
        in_specs=[any_space] * 3,
        out_specs=pl.BlockSpec(memory_space=pltpu.VMEM),
        scratch_shapes=[
            pltpu.VMEM((2 * HALF, 4096), bf16),
            pltpu.VMEM((HALF, HALF), bf16),
            pltpu.VMEM(legs, bf16),
            pltpu.VMEM(legs, bf16),
            pltpu.VMEM(legs, bf16),
            pltpu.VMEM(legs, bf16),
            pltpu.VMEM(legs, bf16),
            pltpu.VMEM((2, 16 * ROWS, HALF), jnp.float32),
            pltpu.VMEM((CHUNKS, PIECES, 4, 4, ROWS, QUARTER), bf16),
            pltpu.VMEM((CHUNKS, PIECES, 2, 4, ROWS, QUARTER), bf16),
            pltpu.VMEM((CHUNKS, PIECES, 4, ROWS, QUARTER), bf16),
            pltpu.VMEM((CHUNKS, PIECES, 2, ROWS, QUARTER), bf16),
            pltpu.VMEM((CHUNKS, PIECES, ROWS, QUARTER), bf16),
            pltpu.SemaphoreType.DMA((2,)),
            pltpu.SemaphoreType.DMA((2, 2, 2, CHUNKS)),
            pltpu.SemaphoreType.DMA((2, 2, 2, CHUNKS)),
            pltpu.SemaphoreType.DMA((CHUNKS, PIECES, 4)),
            pltpu.SemaphoreType.DMA((CHUNKS, PIECES, 4)),
        ],
        compiler_params=pltpu.CompilerParams(
            collective_id=0, has_side_effects=True, vmem_limit_bytes=60 << 20
        ),
    )(hidden.reshape(4, 4, 32, 2 * HALF), down_weight, jnp.asarray(local_rotation()))


def solution(mesh):
    placed = (P("dp", "tensor"), P("tensor", None))
    return jax.shard_map(
        body, mesh=mesh, in_specs=placed, out_specs=P(("dp", "tensor"), None), check_vma=False
    )
```
